1024 devices in a mesh: dp: 64 (over y, x, core), replica: 16 (over z).
Axes of the slice: x: 4, y: 8, z: 16, core: 2. Of those that a mesh axis runs over, the one named last changes fastest.
Arguments:
- tokens: bfloat16 [16, 8192, 1024], P('replica', 'dp'), may hold values from -16 to 16
- user_of_row: int32 [16, 8192], P('replica'), may hold values from 0 to 255, as said below
- proj_weight: bfloat16 [1024, 1536], replicated
- norm_gain: float32 [512], replicated, may hold values from 0.5 to 1.5
- grad_out: bfloat16 [16, 16384, 512], P('replica', 'dp'), may hold values from -6 to 6
Outputs:
- attended: bfloat16 [16, 16384, 512], P('replica', 'dp')
- grad_tokens: bfloat16 [16, 8192, 1024], P('replica', 'dp')
- grad_weight: float32 [1024, 1536], P('dp')
The draws below stay inside these ranges and needn't reach their ends.
Inputs may be any that keep to these rules, and one draw needn't show every extreme that they name: `user_of_row`: user u belongs to owner u // 4. Among the 128 rows of one source device in one batch at most 4 belong to users of any one owner, and in every batch one owner gets exactly 4 rows from every source.
All inputs are finite; a program needn't handle non-finite values.
Results may differ from the reference program's by a relative error of at most 0.0068.
Values may be sent and summed in bfloat16 or wider, within the bound.
A program may use at most 64 MiB of HBM per device.

```python
import math
import jax
import jax.numpy as jnp
from jax import lax

D = 1024
HEADS = 4
HEAD_DIM = 128
UPO = 4
TOK_DEV = 128
HW = 512
QKV = 1536
SOURCES = 64
REPLICAS = 16
CAP = 4
SLOTS = 256
ROWS = 8192
PACKED = 16384


def draw_user_of_row(key, part):
    subkeys = jax.random.split(key, 3)
    hot_owner = jax.random.randint(subkeys[0], (REPLICAS, 1, 1), 0, SOURCES)
    source_keys = jax.random.split(subkeys[1], REPLICAS * SOURCES)

    def one_source(source_key):
        first_key, second_key = jax.random.split(source_key)
        others = CAP + jax.random.permutation(first_key, SOURCES * CAP - CAP)[:TOK_DEV - CAP]
        chosen = jnp.concatenate([jnp.arange(CAP, dtype=jnp.int32), others.astype(jnp.int32)])
        return jax.random.permutation(second_key, chosen)
    chosen_all = jax.vmap(one_source)(source_keys).reshape(REPLICAS, SOURCES, TOK_DEV)
    owners = (chosen_all // CAP + hot_owner) % SOURCES
    within = jax.random.randint(subkeys[2], (REPLICAS, SOURCES, TOK_DEV), 0, UPO)
    return (owners * UPO + within).reshape(REPLICAS, ROWS).astype(jnp.int32)


def draw_proj_weight(key, part):
    entry_key, scale_key = jax.random.split(key)
    entries = jax.random.normal(entry_key, (D, QKV), jnp.float32)
    scales = jnp.exp(jax.random.uniform(scale_key, (1, QKV), jnp.float32, math.log(0.35), math.log(3.5)))
    return (entries * scales / math.sqrt(D)).astype(jnp.bfloat16)


def strengthened(array, rng, source, target, parts, factor):
    def block_of(dim):
        return (jnp.arange(array.shape[dim]) // (array.shape[dim] // parts)).reshape((-1,) + (1,) * (array.ndim - 1 - dim))

    first = jax.random.permutation(rng, parts)[block_of(target)]
    other_side = (block_of(target) + parts // 2) % parts
    return jnp.where((block_of(source) == first) | (block_of(source) == other_side), factor * array, array)


def level_of(key, extent, pieces, least, top_value):
    loudness = 1.0
    for axis_at, parts in pieces:
        draws = jax.random.uniform(jax.random.fold_in(jax.random.fold_in(key, 6), axis_at), (parts,), jnp.float32, least / len(pieces), top_value / len(pieces))
        loudness = loudness * jnp.repeat(jnp.exp(draws), extent[axis_at] // parts).reshape((-1,) + (1,) * (len(extent) - 1 - axis_at))
    return loudness


def normal_values(rng, shape, deviation, bound, cuts=(), held_as=jnp.bfloat16):
    result = deviation * jax.random.normal(rng, shape, jnp.float32)
    if cuts:
        result = result * level_of(rng, shape, cuts, -0.22, 0.18)
    return jnp.clip(result, -bound, bound).astype(held_as)


def noise_with(rng, dims, width, limit, pieces, heavy, kind=jnp.bfloat16):
    array = width * jax.random.normal(rng, dims, jnp.float32)
    if pieces:
        array = array * level_of(rng, dims, pieces, -0.22, 0.18)
    return jnp.clip(strengthened(array, jax.random.fold_in(rng, 3), *heavy), -limit, limit).astype(kind)


def setup_inputs(seed: int = 0) -> dict:
    seeds = jax.random.split(jax.random.key(seed), 6)
    tokens = noise_with(seeds[0], (REPLICAS, ROWS, D), 1.0, 16.0, ((0, 16), (1, 64)), (1, 2, 64, 4.0))
    user_of_row = draw_user_of_row(jax.random.fold_in(seeds[5], 71), 0)
    proj_weight = draw_proj_weight(jax.random.fold_in(seeds[5], 71), 0)
    norm_gain = jnp.clip(1.0 + 0.1 * jax.random.normal(seeds[3], (HW,), jnp.float32), 0.5, 1.5)
    grad_out = normal_values(seeds[4], (REPLICAS, PACKED, HW), 1.0, 6.0, ((0, 16), (1, 64)))
    return {"tokens": tokens, "user_of_row": user_of_row, "proj_weight": proj_weight, "norm_gain": norm_gain, "grad_out": grad_out}


def silu_grad(preact):
    sigmoid_p = jax.nn.sigmoid(preact)
    return sigmoid_p * (1.0 + preact * (1.0 - sigmoid_p))

def attend(activated, gain, slot_user, slot_order):
    slot_total = activated.shape[0]
    split_acts = activated.astype(jnp.float32).reshape(slot_total, 3, HEADS, HEAD_DIM)
    queries = split_acts[:, 0]
    keys_h = split_acts[:, 1]
    values = split_acts[:, 2]
    scores = jnp.einsum('qhd,khd->hqk', queries, keys_h, precision=lax.Precision.HIGHEST) * HEAD_DIM ** (-0.5)
    visible = (slot_user[:, None] == slot_user[None, :]) & (slot_order[None, :] <= slot_order[:, None]) & (slot_user[:, None] >= 0)
    weights = jnp.where(visible[None], jax.nn.silu(scores), 0.0)
    mixed = jnp.einsum('hqk,khd->qhd', weights, values, precision=lax.Precision.HIGHEST).reshape(slot_total, HEADS * HEAD_DIM)
    mean_row = lax.optimization_barrier(jnp.mean(mixed, axis=1, keepdims=True))
    centered = mixed - mean_row
    variance = lax.optimization_barrier(jnp.mean(centered * centered, axis=1, keepdims=True))
    return centered * lax.rsqrt(variance + 1e-06) * gain

def block_pass(activated, gain, slot_user, slot_order, cotangent):

    def forward(acts):
        return attend(acts, gain, slot_user, slot_order)
    normed, pull = jax.vjp(forward, activated)
    d_acts, = pull(cotangent.astype(jnp.float32))
    return (normed.astype(jnp.bfloat16), d_acts)

def reference(tokens, user_of_row, proj_weight, norm_gain, grad_out):
    user_ids = user_of_row.reshape(REPLICAS, SOURCES, TOK_DEV)
    owners = user_ids // UPO
    matches = (owners[..., None] == jnp.arange(SOURCES, dtype=jnp.int32)[None, None, None, :]).astype(jnp.int32)
    in_rank = lax.optimization_barrier(jnp.sum(jnp.cumsum(matches, axis=2) * matches, axis=3)) - 1
    sources_iota = jnp.arange(SOURCES, dtype=jnp.int32)[None, :, None]
    target = (owners * SLOTS + sources_iota * CAP + in_rank).reshape(REPLICAS, ROWS).astype(jnp.int32)
    rows_flat = tokens.reshape(REPLICAS * ROWS, D)
    preact = jnp.dot(rows_flat, proj_weight, preferred_element_type=jnp.float32)
    activated = jax.nn.silu(preact).astype(jnp.bfloat16).reshape(REPLICAS, ROWS, QKV)
    replica_iota = jnp.arange(REPLICAS, dtype=jnp.int32)[:, None]
    packed = jnp.zeros((REPLICAS, PACKED, QKV), activated.dtype).at[replica_iota, target].set(activated)
    slot_user = jnp.full((REPLICAS, PACKED), -1, jnp.int32).at[replica_iota, target].set(user_of_row.astype(jnp.int32))
    order_rows = jnp.broadcast_to(jnp.arange(ROWS, dtype=jnp.int32)[None, :], (REPLICAS, ROWS))
    slot_order = jnp.zeros((REPLICAS, PACKED), jnp.int32).at[replica_iota, target].set(order_rows)

    def one_block(inputs):
        return block_pass(inputs[0], norm_gain, inputs[1], inputs[2], inputs[3])
    attended, d_packed = lax.map(one_block, (packed.reshape(REPLICAS * SOURCES, SLOTS, QKV), slot_user.reshape(REPLICAS * SOURCES, SLOTS), slot_order.reshape(REPLICAS * SOURCES, SLOTS), grad_out.reshape(REPLICAS * SOURCES, SLOTS, HW)))
    d_rows = d_packed.reshape(REPLICAS, PACKED, QKV)[replica_iota, target].reshape(REPLICAS * ROWS, QKV)
    d_rows = lax.optimization_barrier(d_rows)
    d_pre = (d_rows.astype(jnp.float32) * silu_grad(preact)).astype(jnp.bfloat16)
    grad_tokens = jnp.dot(d_pre, proj_weight.T, preferred_element_type=jnp.float32).astype(jnp.bfloat16).reshape(REPLICAS, ROWS, D)
    grad_weight = jnp.dot(rows_flat.T, d_pre, preferred_element_type=jnp.float32)
    return (attended.reshape(REPLICAS, PACKED, HW), grad_tokens, grad_weight)
```

```python
import functools

import jax
import jax.numpy as jnp
from jax import lax
from jax.experimental import pallas as pl
from jax.experimental.pallas import tpu as pltpu
from jax.sharding import PartitionSpec as P

HEADS = 4
HEAD_DIM = 128
MESH = pl.DeviceIdType.MESH
F32 = jnp.float32
BF16 = jnp.bfloat16


def dot(a, b, ca=1, cb=0):
    return lax.dot_general(a, b, (((ca,), (cb,)), ((), ())), preferred_element_type=F32)


def iota(shape, dim):
    return lax.broadcasted_iota(jnp.int32, shape, dim)


def split(x):
    high = x.astype(BF16)
    return high, (x - high.astype(F32)).astype(BF16)


def kernel(
    n, depth, users, tok, gain, w_hbm, gout_hbm, att_hbm, gtok, gw,
    w, gout, att, out1, in1, out2, in2, arrived, slots, pick, pick_t, mix, mix_t, perm,
    turned, turned_in, act, slope, dpre, dpre_in, vis, scores, gates, mixed, dmixed,
    grad, ring_out, ring_in, total, plane_out, plane_in, final,
    load_sem, a2a_send, a2a_recv, pair_send, pair_recv, ring_send, ring_recv, tail_send, tail_recv,
):
    me = lax.axis_index("dp")
    z = lax.axis_index("replica")
    rows, width = tok.shape
    qkv = w.shape[1]
    hw = gout.shape[1]
    core = lax.rem(me, 2)
    chip = me // 2
    chips = n // 2
    half = depth // 2
    partner = me + 1 - 2 * core

    barrier = pltpu.get_barrier_semaphore()

    @pl.loop(1, n)
    def _(k):
        pl.semaphore_signal(barrier, inc=1, device_id=(lax.rem(me + k, n), z), device_id_type=MESH)

    @pl.loop(1, depth)
    def _(k):
        pl.semaphore_signal(barrier, inc=1, device_id=(me, lax.rem(z + k, depth)), device_id_type=MESH)

    load_w = pltpu.make_async_copy(w_hbm, w, load_sem.at[0])
    load_g = pltpu.make_async_copy(gout_hbm, gout, load_sem.at[1])
    load_w.start()
    load_g.start()

    r0, r1 = iota((rows, rows), 0), iota((rows, rows), 1)
    diag = r0 == r1
    owner_row = (users[pl.ds(me, 1), :] >> 2).astype(F32)
    owner_col = jnp.sum(jnp.where(diag, owner_row, 0.0), axis=1, keepdims=True)
    rank = jnp.sum(jnp.where((owner_col == owner_row) & (r0 < r1), 1.0, 0.0), axis=0, keepdims=True)
    place = owner_row * 4.0 + rank
    place_col = jnp.sum(jnp.where(diag, place, 0.0), axis=1, keepdims=True)
    pick[...] = jnp.where(iota((256, rows), 0).astype(F32) == place, 1.0, 0.0).astype(BF16)
    pick_t[...] = jnp.where(iota((rows, 256), 1).astype(F32) == place_col, 1.0, 0.0).astype(BF16)
    m0, m1 = iota((256, 256), 0), iota((256, 256), 1)
    mix[...] = jnp.where(m1 == ((m0 & 63) >> 2) * 16 + (m0 >> 6) * 4 + (m0 & 3), 1.0, 0.0).astype(BF16)
    mix_t[...] = jnp.where(m0 == ((m1 & 63) >> 2) * 16 + (m1 >> 6) * 4 + (m1 & 3), 1.0, 0.0).astype(BF16)

    def unpack(blocks, flat):
        for g in range(4):
            rows_g = dot(mix[...], blocks[g * 16:(g + 1) * 16].reshape(256, 256)).astype(BF16)
            for q in range(4):
                flat[g * 64:(g + 1) * 64, q * 256:(q + 1) * 256] = rows_g[q * 64:(q + 1) * 64]

    def pack(flat, blocks):
        for g in range(4):
            rows_g = jnp.concatenate(
                [flat[g * 64:(g + 1) * 64, q * 256:(q + 1) * 256] for q in range(4)], axis=0
            )
            blocks[g * 16:(g + 1) * 16] = dot(mix_t[...], rows_g).astype(BF16).reshape(16, 16, 256)

    slots[...] = dot(pick[...], tok[...]).astype(BF16)
    pack(slots, out1)

    pl.semaphore_wait(barrier, n - 1 + depth - 1)

    def exchange(source, target, index):
        @pl.loop(1, n)
        def _(k):
            peer = lax.rem(me + k, n)
            pltpu.make_async_remote_copy(
                source.at[peer], target.at[me], a2a_send.at[index], a2a_recv.at[index],
                device_id=(peer, z), device_id_type=MESH,
            ).start()

        target[pl.ds(me, 1)] = source[pl.ds(me, 1)]

    def whole(source, target, sends, recvs, index, count):
        return pltpu.make_async_remote_copy(
            source.at[pl.ds(0, count)], target.at[pl.ds(0, count)], sends.at[index], recvs.at[index],
            device_id=(partner, z), device_id_type=MESH,
        )

    exchange(out1, in1, 0)

    everyone = users[...]
    inbound = jnp.where((everyone >> 2) == me, 1.0, 0.0).astype(BF16)
    upto = jnp.where(r0 <= r1, 1.0, 0.0).astype(BF16)
    count = dot(inbound, upto).astype(BF16)
    spread = jnp.where((iota((256, n), 0) >> 2) == iota((256, n), 1), 1.0, 0.0).astype(BF16)
    nth = ((iota((256, rows), 0) & 3) + 1).astype(F32)
    match = (dot(spread, inbound) > 0.5) & (dot(spread, count) == nth)
    named = dot(spread, (everyone + 1).astype(F32).astype(BF16))
    user_col = jnp.sum(jnp.where(match, named, 0.0), axis=1, keepdims=True) - 1.0
    user_row = jnp.sum(jnp.where(m0 == m1, user_col, 0.0), axis=0, keepdims=True)
    vis[...] = jnp.where((user_col == user_row) & (user_col >= 0.0) & (m1 <= m0), 1.0, 0.0)

    @pl.loop(0, 4)
    def _(t):
        d0 = iota((256, width), 0) + t * 256
        want = (((d0 & 31) * 2 + (d0 >> 9)) << 4) + ((d0 >> 5) & 15)
        perm[pl.ds(pl.multiple_of(t * 256, 256), 256), :] = jnp.where(
            iota((256, width), 1) == want, 1.0, 0.0
        ).astype(BF16)

    load_w.wait()
    load_g.wait()
    whole(out1, in1, a2a_send, a2a_recv, 0, n - 1).wait_recv()
    unpack(in1, arrived)

    @pl.loop(0, 3)
    def _(t):
        cols = pl.ds(pl.multiple_of(t * 512, 512), 512)
        pre = dot(arrived[...], w[:, cols])
        sig = jax.nn.sigmoid(pre)
        act[:, cols] = (pre * sig).astype(BF16)
        slope[:, cols] = sig * (1.0 + pre * (1.0 - sig))

    for t in range(4):
        turned[t // 2, (t % 2) * 256:(t % 2 + 1) * 256, :] = dot(
            perm[t * 256:(t + 1) * 256, :], arrived[...], 1, 1
        ).astype(BF16)
    swap_rows = pltpu.make_async_remote_copy(
        turned.at[1 - core], turned_in, pair_send.at[0], pair_recv.at[0],
        device_id=(partner, z), device_id_type=MESH,
    )
    swap_rows.start()

    scale = HEAD_DIM ** (-0.5)
    seen = vis[...] > 0.5
    for h in range(HEADS):
        q_cols = slice(h * HEAD_DIM, (h + 1) * HEAD_DIM)
        k_cols = slice(hw + h * HEAD_DIM, hw + (h + 1) * HEAD_DIM)
        v_cols = slice(2 * hw + h * HEAD_DIM, 2 * hw + (h + 1) * HEAD_DIM)
        score = dot(act[:, q_cols], act[:, k_cols], 1, 1) * scale
        sig = jax.nn.sigmoid(score)
        weight = jnp.where(seen, score * sig, 0.0)
        scores[h] = weight
        gates[h] = jnp.where(seen, sig * (1.0 + score * (1.0 - sig)) * scale, 0.0)
        high, low = split(weight)
        values = act[:, v_cols]
        mixed[:, q_cols] = dot(high, values) + dot(low, values)

    x = mixed[...]
    center = x - jnp.mean(x, axis=1, keepdims=True)
    scaling = lax.rsqrt(jnp.mean(center * center, axis=1, keepdims=True) + 1e-06)
    hat = center * scaling
    att[...] = (hat * gain[...]).astype(BF16)
    store_att = pltpu.make_async_copy(att, att_hbm, load_sem.at[2])
    store_att.start()
    d_hat = gout[...].astype(F32) * gain[...]
    d_center = scaling * (d_hat - hat * jnp.mean(d_hat * hat, axis=1, keepdims=True))
    dmixed[...] = d_center - jnp.mean(d_center, axis=1, keepdims=True)

    for h in range(HEADS):
        q_cols = slice(h * HEAD_DIM, (h + 1) * HEAD_DIM)
        k_cols = slice(hw + h * HEAD_DIM, hw + (h + 1) * HEAD_DIM)
        v_cols = slice(2 * hw + h * HEAD_DIM, 2 * hw + (h + 1) * HEAD_DIM)
        values = act[:, v_cols]
        m_high, m_low = split(dmixed[:, q_cols])
        d_score = (dot(m_high, values, 1, 1) + dot(m_low, values, 1, 1)) * gates[h]
        s_high, s_low = split(d_score)
        w_high, w_low = split(scores[h])
        keys, queries = act[:, k_cols], act[:, q_cols]
        parts = (
            (q_cols, dot(s_high, keys) + dot(s_low, keys)),
            (k_cols, dot(s_high, queries, 0, 0) + dot(s_low, queries, 0, 0)),
            (v_cols, dot(w_high, m_high, 0, 0) + dot(w_high, m_low, 0, 0) + dot(w_low, m_high, 0, 0)),
        )
        for cols, value in parts:
            dpre[:, cols] = (value.astype(BF16).astype(F32) * slope[:, cols]).astype(BF16)

    swap_dpre = pltpu.make_async_remote_copy(
        dpre, dpre_in, pair_send.at[1], pair_recv.at[1], device_id=(partner, z), device_id_type=MESH
    )
    swap_dpre.start()

    for t in range(4):
        slots[:, t * 256:(t + 1) * 256] = dot(dpre[...], w[t * 256:(t + 1) * 256, :], 1, 1).astype(BF16)
    pack(slots, out2)
    exchange(out2, in2, 1)

    swap_rows.wait()
    swap_dpre.wait()
    column_halves = 2
    wide = qkv // column_halves

    @pl.loop(0, depth // 4)
    def _(b):
        band = pl.ds(pl.multiple_of(b * 4 * chips, 4 * chips), 4 * chips)
        own = turned[pl.ds(core, 1), band, :].reshape(4 * chips, 256)
        other = turned_in[band, :]
        for c in range(column_halves):
            cols = slice(c * wide, (c + 1) * wide)
            block = dot(own, dpre[:, cols]) + dot(other, dpre_in[:, cols])
            grad[pl.ds(b * 4, 4), c] = block.reshape(4, chips, wide)

    def piece(ref, lead, p):
        return ref.at[(*lead, p // 2, pl.ds((p % 2) * 16, 16))]

    def hop(direction, s, p, has_in):
        chunk = lax.rem(z + half - s, depth) if direction == 0 else lax.rem(z + half + s, depth)
        to = lax.rem(z + 1, depth) if direction == 0 else lax.rem(z + depth - 1, depth)
        value = piece(grad, (chunk,), p)[...]
        if has_in:
            arrive(direction, s - 1, p)
            value = value + piece(ring_in, (direction, s - 1), p)[...].astype(F32)
        piece(ring_out, (direction, s), p)[...] = value.astype(BF16)
        pltpu.make_async_remote_copy(
            piece(ring_out, (direction, s), p), piece(ring_in, (direction, s), p),
            ring_send.at[direction, s, p], ring_recv.at[direction, s, p],
            device_id=(me, to), device_id_type=MESH,
        ).start()

    def arrive(direction, s, p):
        pltpu.make_async_remote_copy(
            piece(ring_out, (direction, s), p), piece(ring_in, (direction, s), p),
            ring_send.at[direction, s, p], ring_recv.at[direction, s, p],
            device_id=(me, z), device_id_type=MESH,
        ).wait_recv()

    def sent(direction, s, p):
        pltpu.make_async_remote_copy(
            piece(ring_out, (direction, s), p), piece(ring_in, (direction, s), p),
            ring_send.at[direction, s, p], ring_recv.at[direction, s, p],
            device_id=(me, z), device_id_type=MESH,
        ).wait_send()

    first = ((0, 1), (2, 3))
    for i in range(2):
        for direction in range(2):
            hop(direction, 0, first[direction][i], False)
    for direction in range(2):
        for p in first[1 - direction]:
            hop(direction, 1, p, False)
    for i in range(2):
        for direction in range(2):
            hop(direction, 1, first[direction][i], True)

    @pl.loop(2, half)
    def _(s):
        for p in range(4):
            for direction in range(2):
                hop(direction, s, p, True)

    for p in range(4):
        value = piece(grad, (z,), p)[...]
        for direction in range(2):
            arrive(direction, half - 1, p)
            value = value + piece(ring_in, (direction, half - 1), p)[...].astype(F32)
        total[(p % 2) * 16:(p % 2 + 1) * 16, (p // 2) * wide:(p // 2 + 1) * wide] = value

    for i in range(chips):
        plane_out[i] = total[i:i + 1, :]

    @pl.loop(1, chips)
    def _(k):
        to = lax.rem(chip + k, chips)
        pltpu.make_async_remote_copy(
            plane_out.at[to], plane_in.at[chip], tail_send.at[0], tail_recv.at[0],
            device_id=(to * 2 + core, z), device_id_type=MESH,
        ).start()

    plane_in[pl.ds(chip, 1)] = plane_out[pl.ds(chip, 1)]

    whole(out2, in2, a2a_send, a2a_recv, 1, n - 1).wait_recv()
    unpack(in2, arrived)
    gtok[...] = dot(pick_t[...], arrived[...]).astype(BF16)

    whole(plane_out, plane_in, tail_send, tail_recv, 0, chips - 1).wait_recv()
    row = plane_in[0]
    for i in range(1, chips):
        row = row + plane_in[i]
    final[pl.ds(z, 1)] = row.reshape(1, 1, qkv)

    @pl.loop(1, depth)
    def _(k):
        pltpu.make_async_remote_copy(
            final.at[z], final.at[z], tail_send.at[1], tail_recv.at[1],
            device_id=(me, lax.rem(z + k, depth)), device_id_type=MESH,
        ).start()

    whole(out1, in1, a2a_send, a2a_recv, 0, n - 1).wait_send()
    whole(out2, in2, a2a_send, a2a_recv, 1, n - 1).wait_send()
    whole(plane_out, plane_in, tail_send, tail_recv, 0, chips - 1).wait_send()
    for direction in range(2):
        for p in first[direction]:
            sent(direction, 0, p)

    @pl.loop(1, half)
    def _(s):
        for direction in range(2):
            for p in range(4):
                sent(direction, s, p)

    store_att.wait()
    whole(final, final, tail_send, tail_recv, 1, depth - 1).wait()
    for i in range(depth):
        gw[i:i + 1, :] = final[i]


def body(tokens, user_of_row, proj_weight, norm_gain, grad_out):
    n = lax.axis_size("dp")
    depth = lax.axis_size("replica")
    rows, width = tokens.shape[1:]
    qkv = proj_weight.shape[1]
    slots, hw = grad_out.shape[1:]
    chips, half = n // 2, depth // 2
    vmem = pl.BlockSpec(memory_space=pltpu.VMEM)
    anywhere = pl.BlockSpec(memory_space=pl.ANY)
    blocks = pltpu.VMEM((n, 16, 256), BF16)
    ring = pltpu.VMEM((2, half, 2, chips, qkv // 2), BF16)
    dma = pltpu.SemaphoreType.DMA
    attended, grad_tokens, grad_weight = pl.pallas_call(
        functools.partial(kernel, n, depth),
        out_shape=(
            jax.ShapeDtypeStruct((slots, hw), BF16),
            jax.ShapeDtypeStruct((rows, width), BF16),
            jax.ShapeDtypeStruct((width // n, qkv), F32),
        ),
        in_specs=[vmem, vmem, vmem, anywhere, anywhere],
        out_specs=(anywhere, vmem, vmem),
        scratch_shapes=[
            pltpu.VMEM((width, qkv), BF16),
            pltpu.VMEM((slots, hw), BF16),
            pltpu.VMEM((slots, hw), BF16),
            blocks, blocks, blocks, blocks,
            pltpu.VMEM((slots, width), BF16),
            pltpu.VMEM((slots, width), BF16),
            pltpu.VMEM((slots, rows), BF16),
            pltpu.VMEM((rows, slots), BF16),
            pltpu.VMEM((256, 256), BF16),
            pltpu.VMEM((256, 256), BF16),
            pltpu.VMEM((width, width), BF16),
            pltpu.VMEM((2, width // 2, slots), BF16),
            pltpu.VMEM((width // 2, slots), BF16),
            pltpu.VMEM((slots, qkv), BF16),
            pltpu.VMEM((slots, qkv), F32),
            pltpu.VMEM((slots, qkv), BF16),
            pltpu.VMEM((slots, qkv), BF16),
            pltpu.VMEM((slots, slots), F32),
            pltpu.VMEM((HEADS, slots, slots), F32),
            pltpu.VMEM((HEADS, slots, slots), F32),
            pltpu.VMEM((slots, hw), F32),
            pltpu.VMEM((slots, hw), F32),
            pltpu.VMEM((depth, 2, chips, qkv // 2), F32),
            ring, ring,
            pltpu.VMEM((chips, qkv), F32),
            pltpu.VMEM((chips, 1, qkv), F32),
            pltpu.VMEM((chips, 1, qkv), F32),
            pltpu.VMEM((depth, 1, qkv), F32),
            dma((3,)), dma((2,)), dma((2,)), dma((2,)), dma((2,)),
            dma((2, half, 4)), dma((2, half, 4)), dma((2,)), dma((2,)),
        ],
        compiler_params=pltpu.CompilerParams(
            collective_id=0, has_side_effects=True, vmem_limit_bytes=60 * 1024 * 1024
        ),
    )(
        user_of_row.reshape(n, rows),
        tokens[0],
        norm_gain.reshape(1, hw),
        proj_weight,
        grad_out[0],
    )
    return (attended[None], grad_tokens[None], grad_weight)


def solution(mesh):
    return jax.shard_map(
        body,
        mesh=mesh,
        in_specs=(P("replica", "dp", None), P("replica", None), P(), P(), P("replica", "dp", None)),
        out_specs=(P("replica", "dp", None), P("replica", "dp", None), P("dp", None)),
        check_vma=False,
    )
```

```python
import functools

import jax
import jax.numpy as jnp
from jax import lax
from jax.experimental import pallas as pl
from jax.experimental.pallas import tpu as pltpu
from jax.sharding import PartitionSpec as P

HEADS = 4
HEAD_DIM = 128
MESH = pl.DeviceIdType.MESH
F32 = jnp.float32
BF16 = jnp.bfloat16


def dot(a, b, ca=1, cb=0):
    return lax.dot_general(a, b, (((ca,), (cb,)), ((), ())), preferred_element_type=F32)


def iota(shape, dim):
    return lax.broadcasted_iota(jnp.int32, shape, dim)


def split(x):
    high = x.astype(BF16)
    return high, (x - high.astype(F32)).astype(BF16)


def kernel(
    n, depth, users_hbm, tok_hbm, gain_hbm, w_hbm, gout_hbm, att, gtok, gw,
    users, tok, gain, w, gout, out1, in1, out2, in2, arrived, slots, pick, pick_t, mix, mix_t, perm,
    turned, turned_in, act, slope, dpre, dpre_in, vis, scores, gates, mixed, dmixed,
    grad, ring_out, ring_in, total, plane_out, plane_in, final,
    load_sem, a2a_send, a2a_recv, pair_send, pair_recv, ring_send, ring_recv, tail_send, tail_recv,
):
    me = lax.axis_index("dp")
    z = lax.axis_index("replica")
    rows, width = tok.shape
    qkv = w.shape[1]
    hw = gout.shape[1]
    core = lax.rem(me, 2)
    chip = me // 2
    chips = n // 2
    half = depth // 2
    partner = me + 1 - 2 * core

    barrier = pltpu.get_barrier_semaphore()

    @pl.loop(1, n)
    def _(k):
        pl.semaphore_signal(barrier, inc=1, device_id=(lax.rem(me + k, n), z), device_id_type=MESH)

    @pl.loop(1, depth)
    def _(k):
        pl.semaphore_signal(barrier, inc=1, device_id=(me, lax.rem(z + k, depth)), device_id_type=MESH)

    pairs = ((users_hbm, users), (tok_hbm, tok), (gain_hbm, gain), (w_hbm, w), (gout_hbm, gout))
    loads = [pltpu.make_async_copy(a, b, load_sem.at[i]) for i, (a, b) in enumerate(pairs)]
    for load in loads:
        load.start()

    loads[0].wait()
    r0, r1 = iota((rows, rows), 0), iota((rows, rows), 1)
    diag = r0 == r1
    owner_row = (users[pl.ds(me, 1), :] >> 2).astype(F32)
    owner_col = jnp.sum(jnp.where(diag, owner_row, 0.0), axis=1, keepdims=True)
    rank = jnp.sum(jnp.where((owner_col == owner_row) & (r0 < r1), 1.0, 0.0), axis=0, keepdims=True)
    place = owner_row * 4.0 + rank
    place_col = jnp.sum(jnp.where(diag, place, 0.0), axis=1, keepdims=True)
    pick[...] = jnp.where(iota((256, rows), 0).astype(F32) == place, 1.0, 0.0).astype(BF16)
    pick_t[...] = jnp.where(iota((rows, 256), 1).astype(F32) == place_col, 1.0, 0.0).astype(BF16)
    m0, m1 = iota((256, 256), 0), iota((256, 256), 1)
    mix[...] = jnp.where(m1 == ((m0 & 63) >> 2) * 16 + (m0 >> 6) * 4 + (m0 & 3), 1.0, 0.0).astype(BF16)
    mix_t[...] = jnp.where(m0 == ((m1 & 63) >> 2) * 16 + (m1 >> 6) * 4 + (m1 & 3), 1.0, 0.0).astype(BF16)

    def unpack(blocks, flat):
        for g in range(4):
            rows_g = dot(mix[...], blocks[g * 16:(g + 1) * 16].reshape(256, 256)).astype(BF16)
            for q in range(4):
                flat[g * 64:(g + 1) * 64, q * 256:(q + 1) * 256] = rows_g[q * 64:(q + 1) * 64]

    def pack(flat, blocks):
        for g in range(4):
            rows_g = jnp.concatenate(
                [flat[g * 64:(g + 1) * 64, q * 256:(q + 1) * 256] for q in range(4)], axis=0
            )
            blocks[g * 16:(g + 1) * 16] = dot(mix_t[...], rows_g).astype(BF16).reshape(16, 16, 256)

    loads[1].wait()
    slots[...] = dot(pick[...], tok[...]).astype(BF16)
    pack(slots, out1)

    pl.semaphore_wait(barrier, n - 1 + depth - 1)

    def exchange(source, target, index, recv):
        @pl.loop(1, n)
        def _(k):
            peer = me ^ (n - k)
            pltpu.make_async_remote_copy(
                source.at[peer], target.at[me], a2a_send.at[index], a2a_recv.at[recv],
                device_id=(peer, z), device_id_type=MESH,
            ).start()

        target[pl.ds(me, 1)] = source[pl.ds(me, 1)]

    def whole(source, target, sends, recvs, index, count):
        return pltpu.make_async_remote_copy(
            source.at[pl.ds(0, count)], target.at[pl.ds(0, count)], sends.at[index], recvs.at[index],
            device_id=(partner, z), device_id_type=MESH,
        )

    near = me // (n // 2)
    exchange(out1, in1, 0, near)

    everyone = users[...]
    inbound = jnp.where((everyone >> 2) == me, 1.0, 0.0).astype(BF16)
    upto = jnp.where(r0 <= r1, 1.0, 0.0).astype(BF16)
    count = dot(inbound, upto).astype(BF16)
    spread = jnp.where((iota((256, n), 0) >> 2) == iota((256, n), 1), 1.0, 0.0).astype(BF16)
    nth = ((iota((256, rows), 0) & 3) + 1).astype(F32)
    match = (dot(spread, inbound) > 0.5) & (dot(spread, count) == nth)
    named = dot(spread, (everyone + 1).astype(F32).astype(BF16))
    user_col = jnp.sum(jnp.where(match, named, 0.0), axis=1, keepdims=True) - 1.0
    user_row = jnp.sum(jnp.where(m0 == m1, user_col, 0.0), axis=0, keepdims=True)
    vis[...] = jnp.where((user_col == user_row) & (user_col >= 0.0) & (m1 <= m0), 1.0, 0.0)

    @pl.loop(0, 4)
    def _(t):
        d0 = iota((256, width), 0) + t * 256
        want = (((d0 & 31) * 2 + (d0 >> 9)) << 4) + ((d0 >> 5) & 15)
        perm[pl.ds(pl.multiple_of(t * 256, 256), 256), :] = jnp.where(
            iota((256, width), 1) == want, 1.0, 0.0
        ).astype(BF16)

    loads[3].wait()

    def project(half_of_plane):
        band = pl.ds(pl.multiple_of(half_of_plane * 128, 128), 128)
        for g in range(2):
            blocks_g = in1[pl.ds(half_of_plane * 32 + g * 16, 16)].reshape(256, 256)
            rows_g = dot(mix[...], blocks_g).astype(BF16)
            to = pl.ds(pl.multiple_of(half_of_plane * 128 + g * 64, 64), 64)
            for q in range(4):
                arrived[to, q * 256:(q + 1) * 256] = rows_g[q * 64:(q + 1) * 64]

        @pl.loop(0, 3)
        def _(t):
            cols = pl.ds(pl.multiple_of(t * 512, 512), 512)
            pre = dot(arrived[band, :], w[:, cols])
            sig = jax.nn.sigmoid(pre)
            act[band, cols] = (pre * sig).astype(BF16)
            slope[band, cols] = sig * (1.0 + pre * (1.0 - sig))

        for t in range(4):
            turned[t // 2, (t % 2) * 256:(t % 2 + 1) * 256, band] = dot(
                perm[t * 256:(t + 1) * 256, :], arrived[band, :], 1, 1
            ).astype(BF16)

    def landed(recv, count):
        pltpu.make_async_remote_copy(
            out1.at[pl.ds(0, count)], in1.at[pl.ds(0, count)], a2a_send.at[0], a2a_recv.at[recv],
            device_id=(partner, z), device_id_type=MESH,
        ).wait_recv()

    landed(1 - near, n // 2)
    project(1 - near)
    landed(near, n // 2 - 1)
    project(near)

    swap_rows = pltpu.make_async_remote_copy(
        turned.at[1 - core], turned_in, pair_send.at[0], pair_recv.at[0],
        device_id=(partner, z), device_id_type=MESH,
    )
    swap_rows.start()

    scale = HEAD_DIM ** (-0.5)
    seen = vis[...] > 0.5
    for h in range(HEADS):
        q_cols = slice(h * HEAD_DIM, (h + 1) * HEAD_DIM)
        k_cols = slice(hw + h * HEAD_DIM, hw + (h + 1) * HEAD_DIM)
        v_cols = slice(2 * hw + h * HEAD_DIM, 2 * hw + (h + 1) * HEAD_DIM)
        score = dot(act[:, q_cols], act[:, k_cols], 1, 1) * scale
        sig = jax.nn.sigmoid(score)
        weight = jnp.where(seen, score * sig, 0.0)
        scores[h] = weight
        gates[h] = jnp.where(seen, sig * (1.0 + score * (1.0 - sig)) * scale, 0.0)
        high, low = split(weight)
        values = act[:, v_cols]
        mixed[:, q_cols] = dot(high, values) + dot(low, values)

    x = mixed[...]
    center = x - jnp.mean(x, axis=1, keepdims=True)
    scaling = lax.rsqrt(jnp.mean(center * center, axis=1, keepdims=True) + 1e-06)
    hat = center * scaling
    loads[2].wait()
    loads[4].wait()
    att[...] = (hat * gain[...]).astype(BF16)
    d_hat = gout[...].astype(F32) * gain[...]
    d_center = scaling * (d_hat - hat * jnp.mean(d_hat * hat, axis=1, keepdims=True))
    dmixed[...] = d_center - jnp.mean(d_center, axis=1, keepdims=True)

    swaps = [swap_rows]
    for h in range(HEADS):
        q_cols = slice(h * HEAD_DIM, (h + 1) * HEAD_DIM)
        k_cols = slice(hw + h * HEAD_DIM, hw + (h + 1) * HEAD_DIM)
        v_cols = slice(2 * hw + h * HEAD_DIM, 2 * hw + (h + 1) * HEAD_DIM)
        values = act[:, v_cols]
        m_high, m_low = split(dmixed[:, q_cols])
        d_score = (dot(m_high, values, 1, 1) + dot(m_low, values, 1, 1)) * gates[h]
        s_high, s_low = split(d_score)
        w_high, w_low = split(scores[h])
        keys, queries = act[:, k_cols], act[:, q_cols]
        parts = (
            (q_cols, dot(s_high, keys) + dot(s_low, keys)),
            (k_cols, dot(s_high, queries, 0, 0) + dot(s_low, queries, 0, 0)),
            (v_cols, dot(w_high, m_high, 0, 0) + dot(w_high, m_low, 0, 0) + dot(w_low, m_high, 0, 0)),
        )
        for cols, value in parts:
            dpre[:, cols] = (value.astype(BF16).astype(F32) * slope[:, cols]).astype(BF16)
            swap = pltpu.make_async_remote_copy(
                dpre.at[:, cols], dpre_in.at[:, cols],
                pair_send.at[len(swaps)], pair_recv.at[len(swaps)],
                device_id=(partner, z), device_id_type=MESH,
            )
            swap.start()
            swaps.append(swap)

    def back(t):
        slots[:, t * 256:(t + 1) * 256] = dot(dpre[...], w[t * 256:(t + 1) * 256, :], 1, 1).astype(BF16)

    back(0)
    for swap in swaps:
        swap.wait()
    wide = qkv // 2
    quarter = qkv // 4

    def product(b):
        band = pl.ds(pl.multiple_of(b * 4 * chips, 4 * chips), 4 * chips)
        own = turned[pl.ds(core, 1), band, :].reshape(4 * chips, 256)
        other = turned_in[band, :]
        for c in range(2):
            cols = slice(c * wide, (c + 1) * wide)
            block = dot(own, dpre[:, cols]) + dot(other, dpre_in[:, cols])
            for i in range(2):
                part = block[:, i * quarter:(i + 1) * quarter]
                grad[pl.ds(b * 4, 4), 2 * c + i] = part.reshape(4, chips, quarter)

    def piece(ref, lead, p):
        return ref.at[(*lead, p // 2, pl.ds((p % 2) * 16, 16))]

    def hop(direction, s, p, has_in):
        chunk = lax.rem(z + half - s, depth) if direction == 0 else lax.rem(z + half + s, depth)
        to = lax.rem(z + 1, depth) if direction == 0 else lax.rem(z + depth - 1, depth)
        value = piece(grad, (chunk,), p)[...]
        if has_in:
            arrive(direction, s - 1, p)
            value = value + piece(ring_in, (direction, s - 1), p)[...].astype(F32)
        piece(ring_out, (direction, s), p)[...] = value.astype(BF16)
        pltpu.make_async_remote_copy(
            piece(ring_out, (direction, s), p), piece(ring_in, (direction, s), p),
            ring_send.at[direction, s, p], ring_recv.at[direction, s, p],
            device_id=(me, to), device_id_type=MESH,
        ).start()

    def arrive(direction, s, p):
        pltpu.make_async_remote_copy(
            piece(ring_out, (direction, s), p), piece(ring_in, (direction, s), p),
            ring_send.at[direction, s, p], ring_recv.at[direction, s, p],
            device_id=(me, z), device_id_type=MESH,
        ).wait_recv()

    def sent(direction, s, p):
        pltpu.make_async_remote_copy(
            piece(ring_out, (direction, s), p), piece(ring_in, (direction, s), p),
            ring_send.at[direction, s, p], ring_recv.at[direction, s, p],
            device_id=(me, z), device_id_type=MESH,
        ).wait_send()

    first = ((0, 1, 2, 3), (4, 5, 6, 7))
    head = lax.rem(z + half, depth) // 4
    product(head)
    for i in range(4):
        for direction in range(2):
            hop(direction, 0, first[direction][i], False)

    @pl.loop(1, depth // 4)
    def _(i):
        product(lax.rem(head + i, depth // 4))

    for i in range(4):
        for direction in range(2):
            hop(direction, 1, first[1 - direction][i], False)
    for t in range(1, 4):
        back(t)
    pack(slots, out2)
    exchange(out2, in2, 1, 2)
    for i in range(4):
        for direction in range(2):
            hop(direction, 1, first[direction][i], True)

    @pl.loop(2, half)
    def _(s):
        for p in range(8):
            for direction in range(2):
                hop(direction, s, p, True)

    for p in range(8):
        value = piece(grad, (z,), p)[...]
        for direction in range(2):
            arrive(direction, half - 1, p)
            value = value + piece(ring_in, (direction, half - 1), p)[...].astype(F32)
        total[(p % 2) * 16:(p % 2 + 1) * 16, (p // 2) * quarter:(p // 2 + 1) * quarter] = value

    for i in range(chips):
        plane_out[i] = total[i:i + 1, :]

    @pl.loop(1, chips)
    def _(k):
        to = lax.rem(chip + k, chips)
        pltpu.make_async_remote_copy(
            plane_out.at[to], plane_in.at[chip], tail_send.at[0], tail_recv.at[0],
            device_id=(to * 2 + core, z), device_id_type=MESH,
        ).start()

    plane_in[pl.ds(chip, 1)] = plane_out[pl.ds(chip, 1)]

    pltpu.make_async_remote_copy(
        out2.at[pl.ds(0, n - 1)], in2.at[pl.ds(0, n - 1)], a2a_send.at[1], a2a_recv.at[2],
        device_id=(partner, z), device_id_type=MESH,
    ).wait_recv()
    unpack(in2, arrived)
    gtok[...] = dot(pick_t[...], arrived[...]).astype(BF16)

    whole(plane_out, plane_in, tail_send, tail_recv, 0, chips - 1).wait_recv()
    row = plane_in[0]
    for i in range(1, chips):
        row = row + plane_in[i]
    final[pl.ds(z, 1)] = row.reshape(1, 1, qkv)

    @pl.loop(1, depth)
    def _(k):
        pltpu.make_async_remote_copy(
            final.at[z], final.at[z], tail_send.at[1], tail_recv.at[1],
            device_id=(me, lax.rem(z + k, depth)), device_id_type=MESH,
        ).start()

    whole(out1, in1, a2a_send, a2a_recv, 0, n - 1).wait_send()
    whole(out2, in2, a2a_send, a2a_recv, 1, n - 1).wait_send()
    whole(plane_out, plane_in, tail_send, tail_recv, 0, chips - 1).wait_send()
    for direction in range(2):
        for p in first[direction]:
            sent(direction, 0, p)

    @pl.loop(1, half)
    def _(s):
        for direction in range(2):
            for p in range(8):
                sent(direction, s, p)

    whole(final, final, tail_send, tail_recv, 1, depth - 1).wait()
    for i in range(depth):
        gw[i:i + 1, :] = final[i]


def write(a, b, c, a_out, b_out, c_out, a_held, b_held, c_held, sem):
    moves = ((a, a_held, a_out), (b, b_held, b_out), (c, c_held, c_out))
    loads = [pltpu.make_async_copy(x, y, sem.at[0, i]) for i, (x, y, _) in enumerate(moves)]
    stores = [pltpu.make_async_copy(y, x, sem.at[1, i]) for i, (_, y, x) in enumerate(moves)]
    for load in loads:
        load.start()
    for load, store in zip(loads, stores):
        load.wait()
        store.start()
    for store in stores:
        store.wait()


def body(tokens, user_of_row, proj_weight, norm_gain, grad_out):
    n = lax.axis_size("dp")
    depth = lax.axis_size("replica")
    rows, width = tokens.shape[1:]
    qkv = proj_weight.shape[1]
    slots, hw = grad_out.shape[1:]
    chips, half = n // 2, depth // 2
    vmem = pl.BlockSpec(memory_space=pltpu.VMEM)
    hbm = pl.BlockSpec(memory_space=pltpu.HBM)
    blocks = pltpu.VMEM((n, 16, 256), BF16)
    ring = pltpu.VMEM((2, half, 4, chips, qkv // 4), BF16)
    dma = pltpu.SemaphoreType.DMA
    results = (
        jax.ShapeDtypeStruct((slots, hw), BF16),
        jax.ShapeDtypeStruct((rows, width), BF16),
        jax.ShapeDtypeStruct((width // n, qkv), F32),
    )
    made = pl.pallas_call(
        functools.partial(kernel, n, depth),
        out_shape=results,
        in_specs=[hbm] * 5,
        out_specs=(vmem,) * 3,
        scratch_shapes=[
            pltpu.VMEM((n, rows), jnp.int32),
            pltpu.VMEM((rows, width), BF16),
            pltpu.VMEM((1, hw), F32),
            pltpu.VMEM((width, qkv), BF16),
            pltpu.VMEM((slots, hw), BF16),
            blocks, blocks, blocks, blocks,
            pltpu.VMEM((slots, width), BF16),
            pltpu.VMEM((slots, width), BF16),
            pltpu.VMEM((slots, rows), BF16),
            pltpu.VMEM((rows, slots), BF16),
            pltpu.VMEM((256, 256), BF16),
            pltpu.VMEM((256, 256), BF16),
            pltpu.VMEM((width, width), BF16),
            pltpu.VMEM((2, width // 2, slots), BF16),
            pltpu.VMEM((width // 2, slots), BF16),
            pltpu.VMEM((slots, qkv), BF16),
            pltpu.VMEM((slots, qkv), F32),
            pltpu.VMEM((slots, qkv), BF16),
            pltpu.VMEM((slots, qkv), BF16),
            pltpu.VMEM((slots, slots), F32),
            pltpu.VMEM((HEADS, slots, slots), F32),
            pltpu.VMEM((HEADS, slots, slots), F32),
            pltpu.VMEM((slots, hw), F32),
            pltpu.VMEM((slots, hw), F32),
            pltpu.VMEM((depth, 4, chips, qkv // 4), F32),
            ring, ring,
            pltpu.VMEM((chips, qkv), F32),
            pltpu.VMEM((chips, 1, qkv), F32),
            pltpu.VMEM((chips, 1, qkv), F32),
            pltpu.VMEM((depth, 1, qkv), F32),
            dma((5,)), dma((2,)), dma((3,)), dma((1 + 3 * HEADS,)), dma((1 + 3 * HEADS,)),
            dma((2, half, 8)), dma((2, half, 8)), dma((2,)), dma((2,)),
        ],
        compiler_params=pltpu.CompilerParams(
            collective_id=0, has_side_effects=True, vmem_limit_bytes=66300000
        ),
    )(
        user_of_row.reshape(n, rows),
        tokens[0],
        norm_gain.reshape(1, hw),
        proj_weight,
        grad_out[0],
    )
    attended, grad_tokens, grad_weight = pl.pallas_call(
        write,
        out_shape=results,
        in_specs=[hbm] * 3,
        out_specs=(hbm,) * 3,
        scratch_shapes=[pltpu.VMEM(r.shape, r.dtype) for r in results] + [dma((2, 3))],
        compiler_params=pltpu.CompilerParams(vmem_limit_bytes=66300000),
    )(*made)
    return (attended[None], grad_tokens[None], grad_weight)


def solution(mesh):
    return jax.shard_map(
        body,
        mesh=mesh,
        in_specs=(P("replica", "dp", None), P("replica", None), P(), P(), P("replica", "dp", None)),
        out_specs=(P("replica", "dp", None), P("replica", "dp", None), P("dp", None)),
        check_vma=False,
    )
```
